32 devices in a mesh: img: 4 (over z), seq: 8 (over y, x, core).
Axes of the slice: x: 2, y: 2, z: 4, core: 2. Of those that a mesh axis runs over, the one named last changes fastest.
Arguments:
- activations: bfloat16 [8, 704, 1024], P('img', 'seq'), may hold values from -6 to 6
- valid_keys: int32 [8], P('img'), may hold values from 353 to 704, as said below
- cotangent: bfloat16 [8, 704, 1024], P('img', 'seq'), may hold values from -6 to 6
- norm1_gain: bfloat16 [2, 1024], P(None, 'seq'), may hold values from 0.5 to 1.5
- norm1_bias: bfloat16 [2, 1024], P(None, 'seq'), may hold values from -3 to 3
- w_qkv: bfloat16 [2, 1024, 3072], P(None, 'seq'), may hold values from -0.25 to 0.25
- q_bias: bfloat16 [2, 1024], P(None, 'seq'), may hold values from -3 to 3
- v_bias: bfloat16 [2, 1024], P(None, 'seq'), may hold values from -3 to 3
- w_out: bfloat16 [2, 1024, 1024], P(None, 'seq'), may hold values from -0.1875 to 0.1875
- out_bias: bfloat16 [2, 1024], P(None, 'seq'), may hold values from -3 to 3
- norm2_gain: bfloat16 [2, 1024], P(None, 'seq'), may hold values from 0.5 to 1.5
- norm2_bias: bfloat16 [2, 1024], P(None, 'seq'), may hold values from -3 to 3
- w_up: bfloat16 [2, 1024, 4096], P(None, 'seq'), may hold values from -0.1875 to 0.1875
- up_bias: bfloat16 [2, 4096], P(None, 'seq'), may hold values from -3 to 3
- w_down: bfloat16 [2, 4096, 1024], P(None, 'seq'), may hold values from -0.09375 to 0.09375
- down_bias: bfloat16 [2, 1024], P(None, 'seq'), may hold values from -3 to 3
Outputs:
- output: bfloat16 [8, 704, 1024], P('img', 'seq')
- input_grad: float32 [8, 704, 1024], P('img', 'seq')
- norm1_gain_grad: float32 [2, 1024], P(None, 'seq')
- norm1_bias_grad: float32 [2, 1024], P(None, 'seq')
- w_qkv_grad: float32 [2, 1024, 3072], P(None, 'seq')
- q_bias_grad: float32 [2, 1024], P(None, 'seq')
- v_bias_grad: float32 [2, 1024], P(None, 'seq')
- w_out_grad: float32 [2, 1024, 1024], P(None, 'seq')
- out_bias_grad: float32 [2, 1024], P(None, 'seq')
- norm2_gain_grad: float32 [2, 1024], P(None, 'seq')
- norm2_bias_grad: float32 [2, 1024], P(None, 'seq')
- w_up_grad: float32 [2, 1024, 4096], P(None, 'seq')
- up_bias_grad: float32 [2, 4096], P(None, 'seq')
- w_down_grad: float32 [2, 4096, 1024], P(None, 'seq')
- down_bias_grad: float32 [2, 1024], P(None, 'seq')
The draws below stay inside these ranges and needn't reach their ends.
Inputs may be any that keep to these rules, and one draw needn't show every extreme that they name: `valid_keys`: each image has between half its padded length plus one and all 704 tokens valid; in every draw some image has all 704 valid.
All inputs are finite; a program needn't handle non-finite values.
Results may differ from the reference program's by a relative error of at most 0.023.
Values may be sent and summed in bfloat16 or wider, within the bound.
No kernel may reach another device: no remote copies, remote signals or barrier semaphores. Data moves between devices by JAX's collectives and lax.ppermute only.
A program may use at most 384 MiB of HBM per device.

```python
import jax
import jax.numpy as jnp
from jax import lax

D = 1024
H = 16
HD = 64
FF = 4096
LAYERS = 2
TOK_DEV = 88
IMG_DEV = 2
L = 704
IMGS = 8
QBLOCK = 176
N_IMG = 4
N_SEQ = 8


def draw_valid_keys(key, part):
    seq_len = TOK_DEV * N_SEQ
    images = IMG_DEV * N_IMG
    left_key, right_key = jax.random.split(jax.random.fold_in(key, 11))
    counts = jax.random.randint(left_key, (images,), seq_len // 2 + 1, seq_len + 1)
    chosen = jax.random.randint(right_key, (), 0, images)
    return jnp.where(jnp.arange(images) == chosen, seq_len, counts).astype(jnp.int32)


def levels(key, shape, cuts, smallest, high):
    def one(axis_at, parts):
        steps = jax.random.uniform(jax.random.fold_in(jax.random.fold_in(key, 6), axis_at), (parts,), jnp.float32, smallest / len(cuts), high / len(cuts))
        return jnp.repeat(jnp.exp(steps), shape[axis_at] // parts).reshape((-1,) + (1,) * (len(shape) - axis_at - 1))

    gain = one(*cuts[0])
    for cut in cuts[1:]:
        gain = gain * one(*cut)
    return gain


def centred(own_key, shape, width, limit, cuts=(), kind=jnp.bfloat16):
    factor_of = levels(own_key, shape, cuts, -0.22, 0.18) if cuts else 1.0
    values = jax.random.normal(own_key, shape, jnp.float32) * width * factor_of
    return jnp.minimum(jnp.maximum(values, -limit), limit).astype(kind)


def setup_inputs(seed: int = 0) -> dict:
    seeds = jax.random.split(jax.random.key(seed), 17)
    return {
        "activations": centred(seeds[0], (IMGS, L, D), 1.0, 6.0, ((0, 4), (1, 8))),
        "valid_keys": draw_valid_keys(jax.random.fold_in(seeds[16], 71), 0),
        "cotangent": centred(seeds[2], (IMGS, L, D), 1.0, 6.0, ((0, 4), (1, 8))),
        "norm1_gain": jnp.clip(1.0 + 0.1 * jax.random.normal(seeds[3], (LAYERS, D), jnp.float32), 0.5, 1.5).astype(jnp.bfloat16),
        "norm1_bias": centred(seeds[4], (LAYERS, D), 0.5, 3.0, ((1, 8),)),
        "w_qkv": centred(seeds[5], (LAYERS, D, 3 * D), (D // 2) ** -0.5, 0.25, ((1, 8),)),
        "q_bias": centred(seeds[6], (LAYERS, D), 0.5, 3.0, ((1, 8),)),
        "v_bias": centred(seeds[7], (LAYERS, D), 0.5, 3.0, ((1, 8),)),
        "w_out": centred(seeds[8], (LAYERS, D, D), D ** -0.5, 0.1875, ((1, 8),)),
        "out_bias": centred(seeds[9], (LAYERS, D), 0.5, 3.0, ((1, 8),)),
        "norm2_gain": jnp.clip(1.0 + 0.1 * jax.random.normal(seeds[10], (LAYERS, D), jnp.float32), 0.5, 1.5).astype(jnp.bfloat16),
        "norm2_bias": centred(seeds[11], (LAYERS, D), 0.5, 3.0, ((1, 8),)),
        "w_up": centred(seeds[12], (LAYERS, D, FF), D ** -0.5, 0.1875, ((1, 8),)),
        "up_bias": centred(seeds[13], (LAYERS, FF), 0.5, 3.0, ((1, 8),)),
        "w_down": centred(seeds[14], (LAYERS, FF, D), FF ** -0.5, 0.09375, ((1, 8),)),
        "down_bias": centred(seeds[15], (LAYERS, D), 0.5, 3.0, ((1, 8),)),
    }


EPSILON = 1e-06
MASKED = -1e+30

@jax.custom_vjp
def low(v):
    return lax.optimization_barrier(v.astype(jnp.bfloat16)).astype(jnp.float32)

@jax.custom_vjp
def low_back(v):
    return v

def low_keep(v):
    return (low(v), None)

def low_pass(kept, grad):
    return (grad,)

def back_keep(v):
    return (v, None)

def back_low(kept, grad):
    return (low(grad),)
low.defvjp(low_keep, low_pass)
low_back.defvjp(back_keep, back_low)

def highest(left, right):
    return jnp.dot(left, right, precision=lax.Precision.HIGHEST, preferred_element_type=jnp.float32)

def layer_norm(stream, scaling, shifting):
    center = lax.optimization_barrier(jnp.mean(stream, -1, keepdims=True))
    shifted = stream - center
    spread = lax.optimization_barrier(jnp.mean(shifted * shifted, -1, keepdims=True))
    return shifted * lax.rsqrt(spread + EPSILON) * scaling + shifting

def attention(query, keys, values, key_limit):
    seq_len = query.shape[0]
    counted = jnp.arange(seq_len, dtype=jnp.int32) < key_limit
    blocks = query.reshape(seq_len // QBLOCK, QBLOCK, H, HD)

    def one_block(q_block):
        scores = jnp.einsum('qhd,khd->hqk', q_block, keys, precision=lax.Precision.HIGHEST) * HD ** (-0.5)
        scores = low_back(scores)
        scores = jnp.where(counted[None, None, :], scores, MASKED)
        maximum = lax.optimization_barrier(jnp.max(scores, -1, keepdims=True))
        expsum = jnp.exp(scores - maximum)
        probs = low(expsum / lax.optimization_barrier(jnp.sum(expsum, -1, keepdims=True)))
        return jnp.einsum('hqk,khd->qhd', probs, values, precision=lax.Precision.HIGHEST)
    return lax.map(jax.checkpoint(one_block), blocks).reshape(seq_len, H * HD)

def forward(weights, stream, key_limit):
    gain_one, shift_one, mat_qkv, bias_query, bias_value, mat_out, bias_out, gain_two, shift_two, mat_up, bias_up, mat_down, bias_down = weights
    for layer_index in range(LAYERS):
        normed = low(layer_norm(stream, gain_one[layer_index], shift_one[layer_index]))
        project = highest(normed, mat_qkv[layer_index])
        query = low_back(low(project[:, :D] + bias_query[layer_index])).reshape(-1, H, HD)
        keys = low_back(low(project[:, D:2 * D])).reshape(-1, H, HD)
        values = low_back(low(project[:, 2 * D:] + bias_value[layer_index])).reshape(-1, H, HD)
        attended = low_back(low(attention(query, keys, values, key_limit)))
        middle = stream + low_back(highest(attended, mat_out[layer_index]) + bias_out[layer_index])
        normed_two = low(layer_norm(middle, gain_two[layer_index], shift_two[layer_index]))
        preact = low_back(highest(normed_two, mat_up[layer_index]) + bias_up[layer_index])
        activated = low(jax.nn.gelu(preact, approximate=False))
        stream = middle + low_back(highest(activated, mat_down[layer_index]) + bias_down[layer_index])
    return stream

def reference(activations, valid_keys, cotangent, norm1_gain, norm1_bias, w_qkv, q_bias, v_bias, w_out, out_bias, norm2_gain, norm2_bias, w_up, up_bias, w_down, down_bias):
    weights = tuple((tensor.astype(jnp.float32) for tensor in (norm1_gain, norm1_bias, w_qkv, q_bias, v_bias, w_out, out_bias, norm2_gain, norm2_bias, w_up, up_bias, w_down, down_bias)))

    def per_image(running, sample):
        picture, limit_keys, upstream = sample
        result, pullback = jax.vjp(lambda params, inputs: forward(params, inputs, limit_keys), weights, picture.astype(jnp.float32))
        grad_params, grad_input = pullback(upstream.astype(jnp.float32))
        running = jax.tree.map(jnp.add, running, grad_params)
        return (running, (result.astype(jnp.bfloat16), grad_input))
    zeros = jax.tree.map(jnp.zeros_like, weights)
    totals, (output, input_grad) = lax.scan(per_image, zeros, (activations, valid_keys, cotangent))
    return (output, input_grad, totals[0], totals[1], totals[2], totals[3], totals[4], totals[5], totals[6], totals[7], totals[8], totals[9], totals[10], totals[11], totals[12])
```

```python
import functools
import math

import jax
import jax.numpy as jnp
from jax import lax
from jax.experimental import pallas as pl
from jax.experimental.pallas import tpu as pltpu
from jax.sharding import Mesh
from jax.sharding import PartitionSpec as P

H = 16
HD = 64
LAYERS = 2

EPSILON = 1e-06
MASKED = -1e30
HALF_ROOT = 1.0 / math.sqrt(2.0)
DENSITY = 1.0 / math.sqrt(2.0 * math.pi)
F32 = jnp.float32
BF16 = jnp.bfloat16


SEQ = ("hb", "mid", "core")
TP = ("mid", "core")


def normalize(stream):
    center = jnp.mean(stream, -1, keepdims=True)
    shifted = stream - center
    spread = jnp.mean(shifted * shifted, -1, keepdims=True)
    inverse = lax.rsqrt(spread + EPSILON)
    return (shifted * inverse, inverse)


def norm_back(upstream, normed, inverse, scaling):
    scaled = upstream * scaling
    return inverse * (
        scaled
        - jnp.mean(scaled, -1, keepdims=True)
        - normed * jnp.mean(scaled * normed, -1, keepdims=True)
    )


def gelu_slope(preact):
    return (
        0.5 * (1.0 + lax.erf(preact * HALF_ROOT))
        + preact * jnp.exp(-0.5 * preact * preact) * DENSITY
    )


def dot(a, b):
    return jnp.dot(a, b, preferred_element_type=F32)


def dot_nt(a, b):
    return lax.dot_general(a, b, (((1,), (1,)), ((), ())), preferred_element_type=F32)


def dot_tn(a, b):
    return lax.dot_general(a, b, (((0,), (0,)), ((), ())), preferred_element_type=F32)


def swap(a, axis, bit=1):
    n = lax.axis_size(axis)
    return lax.ppermute(a, axis, [(i, i ^ bit) for i in range(n)])


def fwd_kernel(heads, q_ref, k_ref, v_ref, bias_ref, out_ref):
    width = q_ref.shape[-1]
    group = lax.broadcasted_iota(jnp.int32, (1, width), 1) // HD
    q = q_ref[...] * BF16(HD**-0.5)
    k = k_ref[...]
    v = v_ref[...]
    bias = bias_ref[...]
    total = jnp.zeros(q.shape, F32)
    for h in range(heads):
        qh = jnp.where(group == h, q, jnp.zeros_like(q))
        scores = dot_nt(qh, k) + bias
        top = jnp.max(scores, -1, keepdims=True)
        e = jnp.exp(scores - top)
        sums = jnp.sum(e, -1, keepdims=True)
        o = dot(e.astype(BF16), v) * (1.0 / sums)
        total = jnp.where(group == h, o, total)
    out_ref[...] = total.astype(BF16)


def attend_forward(qkv, bias_row, block):
    rows, width3 = qkv.shape
    width = width3 // 3
    heads = width // HD
    flops = 4 * heads * rows * rows * HD
    return pl.pallas_call(
        functools.partial(fwd_kernel, heads),
        grid=(rows // block,),
        in_specs=[
            pl.BlockSpec((block, width), lambda i: (i, 0)),
            pl.BlockSpec((rows, width), lambda i: (0, 1)),
            pl.BlockSpec((rows, width), lambda i: (0, 2)),
            pl.BlockSpec((1, rows), lambda i: (0, 0)),
        ],
        out_specs=pl.BlockSpec((block, width), lambda i: (i, 0)),
        out_shape=jax.ShapeDtypeStruct((rows, width), BF16),
        cost_estimate=pl.CostEstimate(
            flops=flops, bytes_accessed=8 * rows * width, transcendentals=heads * rows * rows
        ),
        name="attend_forward",
    )(qkv, qkv, qkv, bias_row)


def bwd_kernel(heads, q_ref, k_ref, v_ref, g_ref, bias_ref, out_ref, dk_ref, dv_ref):
    step = pl.program_id(0)
    block, width = q_ref.shape
    rows = k_ref.shape[0]
    group = lax.broadcasted_iota(jnp.int32, (1, width), 1) // HD
    q = q_ref[...] * BF16(HD**-0.5)
    k = k_ref[...]
    v = v_ref[...]
    g = g_ref[...]
    bias = jnp.broadcast_to(bias_ref[...], (rows, block))

    @pl.when(step == 0)
    def _():
        dk_ref[...] = jnp.zeros_like(dk_ref)
        dv_ref[...] = jnp.zeros_like(dv_ref)

    dq = jnp.zeros((block, width), F32)
    for h in range(heads):
        qh = jnp.where(group == h, q, jnp.zeros_like(q))
        gh = jnp.where(group == h, g, jnp.zeros_like(g))
        scores = dot_nt(k, qh) + bias
        top = jnp.max(scores, 0, keepdims=True)
        e = jnp.exp(scores - top)
        probs = e * (1.0 / jnp.sum(e, 0, keepdims=True))
        dp = dot_nt(v, gh)
        rowdot = jnp.sum(dp * probs, 0, keepdims=True)
        ds = (probs * (dp - rowdot)).astype(BF16)
        dk_ref[...] += dot(ds, qh)
        dv_ref[...] += dot(probs.astype(BF16), gh)
        dq = jnp.where(group == h, dot_tn(ds, k), dq)
    first = pl.multiple_of(step * block, block)
    out_ref[pl.ds(first, block), :width] = (dq * (HD**-0.5)).astype(BF16)

    @pl.when(step == pl.num_programs(0) - 1)
    def _():
        out_ref[:, width : 2 * width] = dk_ref[...].astype(BF16)
        out_ref[:, 2 * width :] = dv_ref[...].astype(BF16)


def attend_backward(qkv, grad, bias_col, block):
    rows, width3 = qkv.shape
    width = width3 // 3
    heads = width // HD
    return pl.pallas_call(
        functools.partial(bwd_kernel, heads),
        grid=(rows // block,),
        in_specs=[
            pl.BlockSpec((block, width), lambda i: (i, 0)),
            pl.BlockSpec((rows, width), lambda i: (0, 1)),
            pl.BlockSpec((rows, width), lambda i: (0, 2)),
            pl.BlockSpec((block, width), lambda i: (i, 0)),
            pl.BlockSpec((rows, 1), lambda i: (0, 0)),
        ],
        out_specs=pl.BlockSpec((rows, width3), lambda i: (0, 0)),
        out_shape=jax.ShapeDtypeStruct((rows, width3), BF16),
        scratch_shapes=[pltpu.VMEM((rows, width), F32), pltpu.VMEM((rows, width), F32)],
        cost_estimate=pl.CostEstimate(
            flops=10 * heads * rows * rows * HD,
            bytes_accessed=14 * rows * width,
            transcendentals=heads * rows * rows,
        ),
        name="attend_backward",
    )(qkv, qkv, qkv, grad, bias_col)


def body(
    activations,
    valid_keys,
    cotangent,
    norm1_gain,
    norm1_bias,
    w_qkv,
    q_bias,
    v_bias,
    w_out,
    out_bias,
    norm2_gain,
    norm2_bias,
    w_up,
    up_bias,
    w_down,
    down_bias,
):
    images, tokens, width = activations.shape
    n_mid = lax.axis_size("mid")
    n_tp = 2 * n_mid
    n_seq = 2 * n_tp
    n_img = lax.axis_size("img")
    hb = lax.axis_index("hb")
    mid = lax.axis_index("mid")
    core = lax.axis_index("core")
    tp = mid * 2 + core
    part = width // n_seq
    ff = w_down.shape[1] * n_seq
    ff_part = ff // n_seq
    half = 2 * n_mid * tokens
    rows = 2 * half
    block = 4 * tokens

    def ordered(index, own, other, axis=0):
        return jnp.where(
            index == 0,
            jnp.concatenate([own, other], axis),
            jnp.concatenate([other, own], axis),
        )

    def gather_hb(own):
        return ordered(hb, own, swap(own, "hb"))

    def columns_to_owner(mat, pieces):
        depth = mat.shape[0]
        lanes = mat.shape[1] // (pieces * n_tp)
        blocks = mat.reshape(depth, pieces, n_tp, lanes).transpose(2, 0, 1, 3)
        blocks = blocks.reshape(n_tp, depth, pieces * lanes)
        got = lax.all_to_all(blocks, TP, split_axis=0, concat_axis=0, tiled=True)
        return got.reshape(n_tp * depth, pieces * lanes)

    def rows_to_owner(grad, pieces):
        depth = grad.shape[0] // n_tp
        lanes = grad.shape[1] // pieces
        got = lax.all_to_all(
            grad.reshape(n_tp, depth, pieces * lanes), TP, split_axis=0, concat_axis=0, tiled=True
        )
        return got

    def owner_layout(got, pieces):
        depth = got.shape[1]
        lanes = got.shape[2] // pieces
        got = got.reshape(n_tp, depth, pieces, lanes).transpose(1, 2, 0, 3)
        return got.reshape(depth, pieces * n_tp * lanes)

    def reduce_hb(grad):
        parts = grad.reshape((2, grad.shape[0] // 2) + grad.shape[1:])
        keep = lax.dynamic_index_in_dim(parts, hb, 0, keepdims=False)
        send = lax.dynamic_index_in_dim(parts, 1 - hb, 0, keepdims=False)
        return (keep.astype(F32) + swap(send, "hb").astype(F32)).astype(BF16)

    def reduce_img(a):
        if n_img != 4:
            return lax.psum(a, "img")
        place = lax.axis_index("img")
        low = (place == 0) | (place == 3)
        cut = a.shape[0] // 2
        pairs = [(0, 1), (1, 0), (2, 3), (3, 2)]
        keep = jnp.where(low, a[:cut], a[cut:])
        send = jnp.where(low, a[cut:], a[:cut])
        got = lax.ppermute(send, "img", pairs)
        keep = (keep.astype(F32) + got.astype(F32)).astype(BF16)
        got = lax.ppermute(keep, "img", [(0, 3), (3, 0), (1, 2), (2, 1)])
        keep = (keep.astype(F32) + got.astype(F32)).astype(BF16)
        got = lax.ppermute(keep, "img", pairs)
        return jnp.where(
            low, jnp.concatenate([keep, got], 0), jnp.concatenate([got, keep], 0)
        )

    def sum_core(own, other):
        return own + swap(other.astype(BF16), "core").astype(F32)

    def sum_mid(total):
        bit = 1
        while bit < n_mid:
            low = total.astype(BF16)
            total = low.astype(F32) + swap(low, "mid", bit).astype(F32)
            bit *= 2
        return total

    def mine_mid(a):
        parts = a.reshape(2, n_mid, tokens, a.shape[-1])
        return lax.dynamic_index_in_dim(parts, mid, 1, keepdims=False).reshape(
            2 * tokens, a.shape[-1]
        )

    def scatter_mid(total):
        if n_mid != 2:
            return mine_mid(sum_mid(total))
        parts = total.reshape(2, n_mid, tokens, total.shape[-1])
        keep = lax.dynamic_index_in_dim(parts, mid, 1, keepdims=False)
        send = lax.dynamic_index_in_dim(parts, 1 - mid, 1, keepdims=False)
        got = swap(send.astype(BF16), "mid")
        return (keep + got.astype(F32)).reshape(2 * tokens, total.shape[-1])

    def to_tokens(a):
        parts = a.reshape(2, tokens, a.shape[-1])
        own = lax.dynamic_index_in_dim(parts, hb, 0, keepdims=True)
        other = lax.dynamic_index_in_dim(parts, 1 - hb, 0, keepdims=True)
        return ordered(hb, own, swap(other, "hb"))

    def from_tokens(a):
        spread = jnp.broadcast_to(a[:, None], (2, n_mid, tokens, width))
        spread = spread.reshape(2 * n_mid, tokens, width)
        got = lax.all_to_all(spread, ("hb", "mid"), split_axis=0, concat_axis=0, tiled=True)
        return got.reshape(half, width)

    vectors = jnp.concatenate(
        [
            v.reshape(-1, part)
            for v in (
                norm1_gain,
                norm1_bias,
                q_bias,
                v_bias,
                out_bias,
                norm2_gain,
                norm2_bias,
                down_bias,
                up_bias,
            )
        ],
        0,
    )
    vectors = lax.all_gather(vectors, SEQ, axis=0, tiled=False)
    stacked = vectors[:, : 8 * LAYERS].transpose(1, 0, 2)
    own_vectors = lax.dynamic_index_in_dim(
        stacked.reshape(8, LAYERS, 2, n_tp, part), tp, 3, keepdims=False
    ).astype(F32)
    full_vectors = stacked.reshape(8, LAYERS, width).astype(F32)
    ups = vectors[:, 8 * LAYERS :].reshape(2, n_tp, LAYERS, ff_part)
    ups = lax.dynamic_index_in_dim(ups, tp, 1, keepdims=False).astype(F32)

    row = jnp.arange(rows, dtype=jnp.int32)
    which = row // half
    place = row % half
    position = (
        (place // tokens) * 2 + jnp.where(which == 0, core, 1 - core)
    ) * tokens + place % tokens
    limit = lax.dynamic_index_in_dim(valid_keys, hb, 0, keepdims=False)
    key_bias = jnp.where(position < limit, 0.0, MASKED).astype(F32)
    bias_row = key_bias[None, :]
    bias_col = key_bias[:, None]

    stream = from_tokens(activations).astype(F32)
    mats = []
    for l in range(LAYERS):
        mats.append(
            (
                gather_hb(columns_to_owner(w_qkv[l], 6)),
                gather_hb(w_out[l]),
                gather_hb(columns_to_owner(w_up[l], 2)),
                gather_hb(w_down[l]),
            )
        )
    gradient = from_tokens(cotangent).astype(F32)

    saved = []
    for l in range(LAYERS):
        mat_qkv, mat_out, mat_up, mat_down = mats[l]
        gain_one, shift_one, _, _, bias_out, gain_two, shift_two, bias_down = [
            full_vectors[i, l] for i in range(8)
        ]
        bias_qkv = jnp.concatenate(
            [
                own_vectors[2, l].reshape(-1),
                jnp.zeros((2 * part,), F32),
                own_vectors[3, l].reshape(-1),
            ]
        )
        bias_up = ups[:, l].reshape(-1)
        normed_one, inverse_one = normalize(stream)
        own = (normed_one * gain_one + shift_one).astype(BF16)
        hidden_one = jnp.concatenate([own, swap(own, "core")], 0)
        qkv = (dot(hidden_one, mat_qkv) + bias_qkv).astype(BF16)
        attended = attend_forward(qkv, bias_row, block)
        other = dot(attended[half:], mat_out)
        middle = (
            stream + sum_mid(sum_core(dot(attended[:half], mat_out), other)) + bias_out
        )
        normed_two, inverse_two = normalize(middle)
        own = (normed_two * gain_two + shift_two).astype(BF16)
        hidden_two = jnp.concatenate([own, swap(own, "core")], 0)
        preact = dot(hidden_two, mat_up) + bias_up
        activated = jax.nn.gelu(preact, approximate=False).astype(BF16)
        other = dot(activated[half:], mat_down)
        total = sum_core(dot(activated[:half], mat_down), other)
        if l < LAYERS - 1:
            stream = middle + sum_mid(total) + bias_down
        else:
            stream = mine_mid(middle) + scatter_mid(total) + bias_down
        saved.append(
            (
                normed_one,
                inverse_one,
                hidden_one,
                qkv,
                attended,
                normed_two,
                inverse_two,
                hidden_two,
                preact,
                activated,
            )
        )
    output = to_tokens(stream.astype(BF16))

    def place_own(v, count):
        v = v.reshape(count, 2, 1, part)
        here = lax.broadcasted_iota(jnp.int32, (1, 1, n_tp, 1), 2) == tp
        return jnp.where(here, v, 0.0).reshape(count, width)

    sums = [None] * LAYERS
    grads = [None] * LAYERS
    share = 1.0 / n_mid
    for l in reversed(range(LAYERS)):
        (
            normed_one,
            inverse_one,
            hidden_one,
            qkv,
            attended,
            normed_two,
            inverse_two,
            hidden_two,
            preact,
            activated,
        ) = saved[l]
        mat_qkv, mat_out, mat_up, mat_down = mats[l]
        gain_one = full_vectors[0, l]
        gain_two = full_vectors[5, l]
        own = gradient.astype(BF16)
        grad_mlp = jnp.concatenate([own, swap(own, "core")], 0)
        sum_down = jnp.sum(own.astype(F32), 0) * share
        grad_preact = (dot_nt(grad_mlp, mat_down) * gelu_slope(preact)).astype(BF16)
        other = dot_nt(grad_preact[half:], mat_up)
        grad_hidden = sum_mid(sum_core(dot_nt(grad_preact[:half], mat_up), other))
        grad_down = reduce_img(reduce_hb(dot_tn(activated, grad_mlp).astype(BF16)))
        grad_up = reduce_img(
            rows_to_owner(reduce_hb(dot_tn(hidden_two, grad_preact).astype(BF16)), 2)
        )
        sum_up = jnp.sum(grad_preact.astype(F32), 0)
        sum_gain_two = jnp.sum(grad_hidden * normed_two, 0) * share
        sum_shift_two = jnp.sum(grad_hidden, 0) * share
        grad_middle = gradient + norm_back(grad_hidden, normed_two, inverse_two, gain_two)
        own = grad_middle.astype(BF16)
        grad_branch = jnp.concatenate([own, swap(own, "core")], 0)
        sum_out = jnp.sum(own.astype(F32), 0) * share
        grad_attended = dot_nt(grad_branch, mat_out).astype(BF16)
        grad_qkv = attend_backward(qkv, grad_attended, bias_col, block)
        grad_out = reduce_img(reduce_hb(dot_tn(attended, grad_branch).astype(BF16)))
        other = dot_nt(grad_qkv[half:], mat_qkv)
        total = sum_core(dot_nt(grad_qkv[:half], mat_qkv), other)
        grad_mat_qkv = reduce_img(
            rows_to_owner(reduce_hb(dot_tn(hidden_one, grad_qkv).astype(BF16)), 6)
        )
        sum_qkv = jnp.sum(grad_qkv.astype(F32), 0).reshape(3, 2, part)
        if l > 0:
            grad_hidden = sum_mid(total)
            base = grad_middle
            scale = share
        else:
            grad_hidden = scatter_mid(total)
            base = mine_mid(grad_middle)
            normed_one = mine_mid(normed_one)
            inverse_one = mine_mid(inverse_one)
            scale = 1.0
        sum_gain_one = jnp.sum(grad_hidden * normed_one, 0) * scale
        sum_shift_one = jnp.sum(grad_hidden, 0) * scale
        gradient = base + norm_back(grad_hidden, normed_one, inverse_one, gain_one)
        here = lax.broadcasted_iota(jnp.int32, (1, n_tp, 1), 1) == tp
        wide_up = jnp.where(here, sum_up.reshape(2, 1, ff_part), 0.0)
        wide_up = wide_up.reshape(n_seq, ff_part // part, part).transpose(1, 0, 2)
        sums[l] = jnp.concatenate(
            [
                jnp.stack(
                    [
                        sum_gain_one,
                        sum_shift_one,
                        sum_out,
                        sum_gain_two,
                        sum_shift_two,
                        sum_down,
                    ]
                ),
                place_own(jnp.stack([sum_qkv[0], sum_qkv[2]]), 2),
                wide_up.reshape(ff_part // part, width),
            ],
            0,
        )
        grads[l] = (
            owner_layout(grad_mat_qkv, 6),
            grad_out,
            owner_layout(grad_up, 2),
            grad_down,
        )

    input_grad = to_tokens(gradient)

    table = jnp.stack(sums)
    count = table.shape[1]
    spread = table.reshape(LAYERS * count, n_seq, part).transpose(1, 0, 2)
    spread = jnp.broadcast_to(spread[None], (n_img, n_seq, LAYERS * count, part))
    got = lax.all_to_all(
        spread.reshape(n_img * n_seq, LAYERS * count, part),
        ("img",) + SEQ,
        split_axis=0,
        concat_axis=0,
        tiled=True,
    )
    small = jnp.sum(got, 0).reshape(LAYERS, count, part)
    mats_out = [
        jnp.stack([grads[l][i].astype(F32) for l in range(LAYERS)]) for i in range(4)
    ]
    return (
        output,
        input_grad,
        small[:, 0],
        small[:, 1],
        mats_out[0],
        small[:, 6],
        small[:, 7],
        mats_out[1],
        small[:, 2],
        small[:, 3],
        small[:, 4],
        mats_out[2],
        small[:, 8:].reshape(LAYERS, ff_part),
        mats_out[3],
        small[:, 5],
    )


def solution(mesh):
    n_img, n_seq = mesh.devices.shape
    inner = Mesh(
        mesh.devices.reshape(n_img, 2, n_seq // 4, 2), ("img", "hb", "mid", "core")
    )
    tokens = P("img", SEQ, None)
    vector = P(None, SEQ)
    matrix = P(None, SEQ, None)
    return jax.shard_map(
        body,
        mesh=inner,
        in_specs=(
            tokens,
            P("img"),
            tokens,
            vector,
            vector,
            matrix,
            vector,
            vector,
            matrix,
            vector,
            vector,
            vector,
            matrix,
            vector,
            matrix,
            vector,
        ),
        out_specs=(
            tokens,
            tokens,
            vector,
            vector,
            matrix,
            vector,
            vector,
            matrix,
            vector,
            vector,
            vector,
            matrix,
            vector,
            matrix,
            vector,
        ),
        check_vma=False,
    )
```
